32 devices in a mesh: domain: 2 (over core), shard: 16 (over z, y, x).
Axes of the slice: x: 2, y: 2, z: 4, core: 2. Of those that a mesh axis runs over, the one named last changes fastest.
Arguments:
- gradients: bfloat16 [2, 128, 4096], P('domain', 'shard'), may hold values from -64 to 64
- pair_blocks: int32 [2, 2], replicated, may hold values from 0 to 4, as said below
Outputs:
- influence: float32 [2, 128, 48], P('domain', 'shard')
The draws below stay inside these ranges and needn't reach their ends.
Inputs may be any that keep to these rules, and one draw needn't show every extreme that they name: pair_blocks is symmetric; some pair takes 4 blocks in every draw.
All inputs are finite; a program needn't handle non-finite values.
Results may differ from the reference program's by a relative error of at most 0.00039.
Values may be sent and summed in bfloat16 or wider, within the bound.
A program may use at most 64 MiB of HBM per device.

```python
import math
import jax
import jax.numpy as jnp
from jax import lax

BLOCK_WIDTH = 64
FISHER_BLOCKS = 64
EX_DEV = 8
COUNT_MAX = 4
DOMAINS = 2
EXAMPLES = 128
N_SHARD = 16


def draw_gradients(key, part):
    full_width = FISHER_BLOCKS * BLOCK_WIDTH
    key_list = jax.random.split(jax.random.fold_in(key, 11), 3)
    shared_base = jax.random.normal(key_list[0], (full_width,), jnp.float32)
    column_scale = jnp.exp(jax.random.uniform(key_list[1], (full_width,), jnp.float32, math.log(0.5), math.log(2.0)))

    def one_domain(domain_number):
        domain_key = jax.random.fold_in(key_list[2], domain_number)
        noise_key, direction_key, weight_key, scale_key = jax.random.split(domain_key, 4)
        noise = jax.random.normal(noise_key, (EXAMPLES, FISHER_BLOCKS, BLOCK_WIDTH), jnp.float32)
        strength = 0.1
        noise = noise + 0.6 * jnp.roll(noise, 1, axis=2)
        noise = noise.reshape(EXAMPLES, full_width) * column_scale
        direction = 0.7 * shared_base + 0.7 * jax.random.normal(direction_key, (full_width,), jnp.float32)
        weights = jax.random.normal(weight_key, (EXAMPLES, 1), jnp.float32)
        row_scale = jnp.exp(jax.random.uniform(scale_key, (EXAMPLES, 1), jnp.float32, math.log(0.3), math.log(3.0)))
        position = domain_number * EXAMPLES + jnp.arange(EXAMPLES, dtype=jnp.int32)
        rising = jnp.exp(math.log(3.0) * position.astype(jnp.float32) / (DOMAINS * EXAMPLES))
        values = (noise + strength * weights * direction) * row_scale * rising[:, None]
        return jnp.clip(values, -64.0, 64.0).astype(jnp.bfloat16)
    return lax.map(one_domain, jnp.arange(DOMAINS, dtype=jnp.int32))


def draw_pair_blocks(key, part):
    first_key, second_key = jax.random.split(jax.random.fold_in(key, 23))
    drawn = jax.random.randint(first_key, (DOMAINS, DOMAINS), 0, COUNT_MAX + 1, dtype=jnp.int32)
    symmetric = jnp.triu(drawn) + jnp.triu(drawn, 1).T
    picked = jax.random.randint(second_key, (2,), 0, DOMAINS, dtype=jnp.int32)
    index_row = jnp.arange(DOMAINS, dtype=jnp.int32)[:, None]
    index_col = jnp.arange(DOMAINS, dtype=jnp.int32)[None, :]
    chosen = (index_row == picked[0]) & (index_col == picked[1]) | (index_row == picked[1]) & (index_col == picked[0])
    return jnp.where(chosen, COUNT_MAX, symmetric).astype(jnp.int32)


def setup_inputs(seed: int = 0) -> dict:
    arg_keys = jax.random.split(jax.random.key(seed), 3)
    gradients = draw_gradients(jax.random.fold_in(arg_keys[2], 71), 0)
    pair_blocks = draw_pair_blocks(jax.random.fold_in(arg_keys[2], 71), 0)
    return dict(gradients=gradients, pair_blocks=pair_blocks)


damping = 0.5

def invert(statistics, example_total):
    traces = jnp.einsum('bpp->b', statistics)
    order = statistics.shape[-1]
    identity = jnp.eye(order, dtype=jnp.float32)
    fisher = statistics / example_total + (damping * traces / (order * example_total))[:, None, None] * identity
    factor = jnp.linalg.cholesky(fisher)
    identities = jnp.broadcast_to(identity, fisher.shape)
    factor_inv = lax.linalg.triangular_solve(factor, identities, left_side=True, lower=True)
    return jnp.einsum('bkp,bkq->bpq', factor_inv, factor_inv, precision=lax.Precision.HIGHEST)

def reference(gradients, pair_blocks):
    example_total = DOMAINS * EXAMPLES
    full_width = FISHER_BLOCKS * BLOCK_WIDTH

    def shard_rows(shard_number):
        first_row = (shard_number * EX_DEV).astype(jnp.int32)
        return lax.dynamic_slice_in_dim(gradients, first_row, EX_DEV, 1)

    def shard_stats(shard_number):
        blocked = shard_rows(shard_number).astype(jnp.float32).reshape(DOMAINS * EX_DEV, FISHER_BLOCKS, BLOCK_WIDTH)
        return jnp.einsum('ibp,ibq->bpq', blocked, blocked)
    shard_numbers = jnp.arange(N_SHARD, dtype=jnp.int32)
    statistics = lax.optimization_barrier(jnp.sum(lax.map(shard_stats, shard_numbers), axis=0))
    inverse = invert(statistics, example_total)
    inv_root = 1.0 / math.sqrt(full_width)
    row_index = jnp.arange(EX_DEV, dtype=jnp.int32)
    limits = pair_blocks * (EX_DEV // COUNT_MAX)

    def shard_tiles(shard_number):
        own_rows = shard_rows(shard_number)
        blocked = own_rows.astype(jnp.float32).reshape(DOMAINS, EX_DEV, FISHER_BLOCKS, BLOCK_WIDTH)
        precond = jnp.einsum('aibp,bpq->aibq', blocked, inverse, precision=lax.Precision.HIGHEST)
        precond = precond.reshape(DOMAINS, EX_DEV, full_width).astype(jnp.bfloat16)
        targets = jnp.stack([shard_rows(((shard_number + step_by) % N_SHARD).astype(jnp.int32)) for step_by in (-1, 0, 1)], 0)
        raw_tiles = jnp.einsum('aik,ubjk->aiubj', precond.astype(jnp.float32), targets.astype(jnp.float32)) * inv_root
        kept_mask = (row_index[None, :, None, None, None] < limits[:, None, None, :, None]) & (row_index[None, None, None, None, :] < limits[:, None, None, :, None])
        return jnp.where(kept_mask, raw_tiles, 0.0).reshape(DOMAINS, EX_DEV, 3 * DOMAINS * EX_DEV)
    stacked = lax.map(shard_tiles, shard_numbers)
    return jnp.transpose(stacked, (1, 0, 2, 3)).reshape(DOMAINS, EXAMPLES, 3 * DOMAINS * EX_DEV)
```

```python
import functools
import math

import jax
import jax.numpy as jnp
from jax import lax
from jax.experimental import pallas as pl
from jax.experimental.pallas import tpu as pltpu
from jax.sharding import PartitionSpec as P

BLOCK_WIDTH = 64
COUNT_MAX = 4
LANES = 128
STEPS = (-1, 0, 1)


damping = 0.5


def split(value):
    high = value.astype(jnp.bfloat16)
    rest = value - high.astype(jnp.float32)
    middle = rest.astype(jnp.bfloat16)
    low = (rest - middle.astype(jnp.float32)).astype(jnp.bfloat16)
    return high, middle, low


def exact_dot(left, right):
    return jnp.dot(
        left, right, preferred_element_type=jnp.float32, precision=lax.Precision.HIGHEST
    )


def invert_modules(statistics, example_total):
    order = BLOCK_WIDTH
    width = statistics.shape[0]
    row = lax.broadcasted_iota(jnp.int32, (width, width), 0)
    column = lax.broadcasted_iota(jnp.int32, (width, width), 1)
    same = row // order == column // order
    diagonal = row == column
    identity = jnp.where(diagonal, 1.0, 0.0)
    entries = jnp.sum(jnp.where(diagonal, statistics, 0.0), axis=0, keepdims=True)
    lane = lax.broadcasted_iota(jnp.int32, (1, width), 1) // order
    traces = jnp.zeros((1, width), jnp.float32)
    for module in range(width // order):
        here = lane == module
        total = jnp.sum(jnp.where(here, entries, 0.0), axis=1, keepdims=True)
        traces = jnp.where(here, total, traces)
    scale = order / traces
    scaled = jnp.where(same, statistics * scale, 0.0) + damping * identity
    low, high = damping, order + damping
    bound = (high + low) / (high - low)
    residual = identity - (2.0 / (high + low)) * scaled
    now, later = bound, 2.0 * bound * bound - 1.0
    gain = 2.0 * now * now / later
    inverse = (gain * 2.0 / (high + low)) * (identity + residual)
    residual = gain * exact_dot(residual, residual) - (1.0 / later) * identity
    while later < 1e4:
        now, later = later, 2.0 * later * later - 1.0
        gain = 2.0 * now * now / later
        both = exact_dot(jnp.concatenate([inverse, residual], 0), residual)
        inverse = gain * (inverse + both[:width])
        residual = gain * both[width:] - (1.0 / later) * identity
    error = identity - exact_dot(scaled, inverse)
    inverse = inverse + exact_dot(inverse, error)
    return inverse * (scale * example_total)


def kernel(domain_count, shard_count, grads, pairs, out, own, rows_in, tiles_out, tiles_in,
           load_sem, send_sem, recv_sem, send_sem2, recv_sem2):
    devices = domain_count * shard_count
    domain, shard = lax.axis_index("domain"), lax.axis_index("shard")
    here = shard * domain_count + domain
    examples, full_width = own.shape
    width = full_width // devices
    wide = domain_count * examples
    total = devices * examples

    def place(index):
        return {"domain": lax.rem(index, domain_count), "shard": lax.div(index, domain_count)}

    load = pltpu.make_async_copy(grads, own, load_sem)
    load.start()
    others = [lax.rem(here + step, devices) for step in range(1, devices)]
    barrier = pltpu.get_barrier_semaphore()
    for other in others:
        pl.semaphore_signal(
            barrier, inc=1, device_id=place(other), device_id_type=pl.DeviceIdType.MESH
        )
    load.wait()
    mine = pl.ds(pl.multiple_of(here * width, LANES), width)
    rows_in[pl.ds(here, 1)] = own[:, mine][None]
    pl.semaphore_wait(barrier, devices - 1)

    first = []
    for step, other in enumerate(others):
        copy = pltpu.make_async_remote_copy(
            src_ref=own.at[:, pl.ds(pl.multiple_of(other * width, LANES), width)],
            dst_ref=rows_in.at[here],
            send_sem=send_sem.at[step],
            recv_sem=recv_sem.at[step],
            device_id=place(other),
            device_id_type=pl.DeviceIdType.MESH,
        )
        copy.start()
        first.append(copy)
    for copy in first:
        copy.wait()

    rows = rows_in[...].astype(jnp.float32).reshape(total, width).astype(jnp.bfloat16)
    statistics = lax.dot_general(
        rows, rows, (((0,), (0,)), ((), ())), preferred_element_type=jnp.float32
    )
    inverse = invert_modules(statistics, float(total))
    precond = jnp.zeros((total, width), jnp.float32)
    for term in split(inverse)[::-1]:
        precond = precond + jnp.dot(rows, term, preferred_element_type=jnp.float32)
    products = lax.dot_general(
        precond.astype(jnp.bfloat16), rows, (((1,), (1,)), ((), ())),
        preferred_element_type=jnp.float32,
    )
    taken = tiles_out.shape[-1]
    for position in range(shard_count):
        band = products[position * wide:(position + 1) * wide]
        start = (position + STEPS[0]) * wide % total
        band = pltpu.roll(band, (total - start) % total, 1)[:, :taken]
        for number in range(domain_count):
            tiles_out[position * domain_count + number] = band[
                number * examples:(number + 1) * examples
            ]
    tiles_in[pl.ds(here, 1)] = tiles_out[pl.ds(here, 1)]

    second = []
    for step, other in enumerate(others):
        copy = pltpu.make_async_remote_copy(
            src_ref=tiles_out.at[other],
            dst_ref=tiles_in.at[here],
            send_sem=send_sem2.at[step],
            recv_sem=recv_sem2.at[step],
            device_id=place(other),
            device_id_type=pl.DeviceIdType.MESH,
        )
        copy.start()
        second.append(copy)

    column = lax.broadcasted_iota(jnp.int32, (examples, taken), 1)
    column_domain = lax.rem(lax.div(column, examples), domain_count)
    limits = jnp.zeros((examples, taken), jnp.int32)
    for number in range(domain_count):
        limit = pairs[domain, number] * (examples // COUNT_MAX)
        limits = jnp.where(column_domain == number, limit, limits)
    row = lax.broadcasted_iota(jnp.int32, (examples, taken), 0)
    kept = (row < limits) & (lax.rem(column, examples) < limits)
    for copy in second:
        copy.wait()
    influence = jnp.sum(tiles_in[...], axis=0) * (1.0 / math.sqrt(full_width))
    influence = jnp.where(kept, influence, 0.0)
    out[...] = influence[:, :out.shape[-1]]


def fused(gradients, pair_blocks):
    domain_count, shard_count = lax.axis_size("domain"), lax.axis_size("shard")
    devices = domain_count * shard_count
    examples, full_width = gradients.shape[1:]
    width = full_width // devices
    columns = len(STEPS) * domain_count * examples
    taken = pl.cdiv(columns, LANES) * LANES
    dma = pltpu.SemaphoreType.DMA((devices - 1,))
    result = pl.pallas_call(
        functools.partial(kernel, domain_count, shard_count),
        out_shape=jax.ShapeDtypeStruct((examples, columns), jnp.float32),
        in_specs=[
            pl.BlockSpec(memory_space=pl.ANY),
            pl.BlockSpec(memory_space=pltpu.SMEM),
        ],
        out_specs=pl.BlockSpec(memory_space=pltpu.VMEM),
        scratch_shapes=[
            pltpu.VMEM((examples, full_width), gradients.dtype),
            pltpu.VMEM((devices, examples, width), gradients.dtype),
            pltpu.VMEM((devices, examples, taken), jnp.float32),
            pltpu.VMEM((devices, examples, taken), jnp.float32),
            pltpu.SemaphoreType.DMA,
            dma, dma, dma, dma,
        ],
        compiler_params=pltpu.CompilerParams(collective_id=0, has_side_effects=True),
        name="influence",
    )(gradients[0], pair_blocks)
    return result[None]


def shifted(value, axis, steps):
    count = lax.axis_size(axis)
    pairs = [(source, (source + steps) % count) for source in range(count)]
    return lax.ppermute(value, axis, pairs)


def invert(statistics, example_total):
    traces = jnp.einsum("bpp->b", statistics)
    order = statistics.shape[-1]
    identity = jnp.eye(order, dtype=jnp.float32)
    fisher = (
        statistics / example_total
        + (damping * traces / (order * example_total))[:, None, None] * identity
    )
    factor = jnp.linalg.cholesky(fisher)
    identities = jnp.broadcast_to(identity, fisher.shape)
    factor_inv = lax.linalg.triangular_solve(factor, identities, left_side=True, lower=True)
    return jnp.einsum("bkp,bkq->bpq", factor_inv, factor_inv, precision=lax.Precision.HIGHEST)


def local(gradients, pair_blocks):
    own_rows = gradients[0]
    examples_here, full_width = own_rows.shape
    module_count = full_width // BLOCK_WIDTH
    domain_count = lax.axis_size("domain")
    example_total = examples_here * domain_count * lax.axis_size("shard")
    blocked = own_rows.reshape(examples_here, module_count, BLOCK_WIDTH)
    statistics = jnp.einsum("ibp,ibq->bpq", blocked, blocked, preferred_element_type=jnp.float32)
    partial_sum = lax.psum_scatter(statistics, "shard", scatter_dimension=0, tiled=True)
    partial_sum = lax.psum(partial_sum, "domain")
    inverse = lax.all_gather(invert(partial_sum, example_total), "shard", axis=0, tiled=True)
    precond = jnp.einsum(
        "ibp,bpq->ibq", blocked.astype(jnp.float32), inverse, precision=lax.Precision.HIGHEST
    )
    precond = precond.reshape(examples_here, full_width).astype(jnp.bfloat16)
    inv_root = 1.0 / math.sqrt(full_width)
    domain_index = lax.axis_index("domain")
    row_pieces = []
    for step_by in (-1, 0, 1):
        if step_by == 0:
            row_pieces.append(precond)
        else:
            row_pieces.append(shifted(precond, "shard", step_by))
    queries = jnp.concatenate(row_pieces, 0)
    wide = domain_count * examples_here
    direct = (
        jnp.einsum(
            "ik,jk->ij",
            queries,
            lax.all_gather(own_rows, "domain", axis=0, tiled=True),
            preferred_element_type=jnp.float32,
        )
        * inv_root
    )
    row_blocks = direct.reshape(3, examples_here, wide)
    received = []
    for step_by in (-1, 0, 1):
        if step_by == 0:
            received.append(row_blocks[1])
        else:
            received.append(shifted(row_blocks[step_by + 1], "shard", -step_by))
    final = jnp.stack(received, 0)
    raw_tiles = jnp.transpose(final, (1, 0, 2)).reshape(examples_here, 3 * wide)
    counts = lax.dynamic_index_in_dim(pair_blocks, domain_index, 0, keepdims=False)
    column_all = jnp.arange(3 * wide, dtype=jnp.int32)
    column_domain = column_all // examples_here % domain_count
    limits = jnp.take(counts * (examples_here // COUNT_MAX), column_domain)
    column_index = column_all % examples_here
    row_index = jnp.arange(examples_here, dtype=jnp.int32)
    kept_mask = (row_index[:, None] < limits[None, :]) & (column_index < limits)[None, :]
    return jnp.where(kept_mask, raw_tiles, 0.0)[None]


def solution(mesh):
    placed = (P("domain", "shard", None), P())

    def body(gradients, pair_blocks):
        domain_count, shard_count = mesh.shape["domain"], mesh.shape["shard"]
        devices = domain_count * shard_count
        examples, full_width = gradients.shape[1:]
        columns = len(STEPS) * domain_count * examples
        whole_modules = full_width % (devices * math.lcm(LANES, BLOCK_WIDTH)) == 0
        if whole_modules and examples % 8 == 0 and columns <= devices * examples:
            return fused(gradients, pair_blocks)
        return local(gradients, pair_blocks)

    return jax.shard_map(
        body, mesh=mesh, in_specs=placed, out_specs=P("domain", "shard", None), check_vma=False
    )
```

```python
import functools
import math

import jax
import jax.numpy as jnp
from jax import lax
from jax.experimental import pallas as pl
from jax.experimental.pallas import tpu as pltpu
from jax.sharding import PartitionSpec as P

BLOCK_WIDTH = 64
COUNT_MAX = 4
LANES = 128
STEPS = (-1, 0, 1)
OWNER_SHARE = 2


damping = 0.5


def split(value):
    high = value.astype(jnp.bfloat16)
    rest = value - high.astype(jnp.float32)
    middle = rest.astype(jnp.bfloat16)
    low = (rest - middle.astype(jnp.float32)).astype(jnp.bfloat16)
    return high, middle, low


def beside(*parts):
    return jnp.concatenate(parts, axis=1)


def above(*parts):
    return jnp.concatenate(parts, axis=0)


def wide_dot(left, right):
    return jnp.dot(left, right, preferred_element_type=jnp.float32)


def short_dot(left, right):
    width = right.shape[1]
    left_high, left_middle, _ = split(left)
    right_high, right_middle, _ = split(right)
    weights = above(
        beside(right_high, right_middle), beside(right_high, jnp.zeros_like(right_middle))
    )
    both = wide_dot(beside(left_high, left_middle), weights)
    return both[:, :width] + both[:, width:]


def exact_dot(left, right):
    width = right.shape[1]
    left_high, left_middle, left_low = split(left)
    right_high, right_middle, right_low = split(right)
    line = beside(right_high, right_middle)
    both = wide_dot(beside(left_high, left_middle), above(line, line))
    small = wide_dot(beside(left_high, left_low), above(right_low, right_high))
    return both[:, :width] + (both[:, width:] + small)


def invert_modules(groups, example_total):
    order = BLOCK_WIDTH
    width = groups[0].shape[0]
    row = lax.broadcasted_iota(jnp.int32, (width, width), 0)
    column = lax.broadcasted_iota(jnp.int32, (width, width), 1)
    same = row // order == column // order
    diagonal = row == column
    identity = jnp.where(diagonal, 1.0, 0.0)
    lane = lax.broadcasted_iota(jnp.int32, (1, width), 1) // order
    low, high = damping, order + damping
    bound = (high + low) / (high - low)
    scales, scaled, inverses, residuals = [], [], [], []
    now, later = bound, 2.0 * bound * bound - 1.0
    gain = 2.0 * now * now / later
    for statistics in groups:
        entries = jnp.sum(jnp.where(diagonal, statistics, 0.0), axis=0, keepdims=True)
        traces = jnp.zeros((1, width), jnp.float32)
        for module in range(width // order):
            here = lane == module
            total = jnp.sum(jnp.where(here, entries, 0.0), axis=1, keepdims=True)
            traces = jnp.where(here, total, traces)
        scale = order / traces
        matrix = jnp.where(same, statistics * scale, 0.0) + damping * identity
        residual = identity - (2.0 / (high + low)) * matrix
        scales.append(scale)
        scaled.append(matrix)
        inverses.append((gain * 2.0 / (high + low)) * (identity + residual))
        residuals.append(residual)
    products = [short_dot(residual, residual) for residual in residuals]
    residuals = [gain * product - (1.0 / later) * identity for product in products]
    while later < 1e4:
        now, later = later, 2.0 * later * later - 1.0
        gain = 2.0 * now * now / later
        products = [
            short_dot(above(inverse, residual), residual)
            for inverse, residual in zip(inverses, residuals)
        ]
        inverses = [
            gain * (inverse + both[:width]) for inverse, both in zip(inverses, products)
        ]
        residuals = [gain * both[width:] - (1.0 / later) * identity for both in products]
    errors = [
        identity - exact_dot(matrix, inverse) for matrix, inverse in zip(scaled, inverses)
    ]
    products = [short_dot(inverse, error) for inverse, error in zip(inverses, errors)]
    return [
        (inverse + product) * (scale * example_total)
        for inverse, product, scale in zip(inverses, products, scales)
    ]


def influence_tiles(rows, tiles_out, domain_count, shard_count, examples):
    total, width = rows.shape
    wide = domain_count * examples
    statistics = lax.dot_general(
        rows, rows, (((0,), (0,)), ((), ())), preferred_element_type=jnp.float32
    )
    spans = [slice(start, start + LANES) for start in range(0, width, LANES)]
    inverses = invert_modules([statistics[span, span] for span in spans], float(total))
    pieces = []
    for span, inverse in zip(spans, inverses):
        high, middle, low = split(inverse)
        group = rows[:, span]
        piece = wide_dot(beside(group, group), above(high, middle)) + wide_dot(group, low)
        pieces.append(piece.astype(jnp.bfloat16))
    products = lax.dot_general(
        beside(*pieces), rows, (((1,), (1,)), ((), ())), preferred_element_type=jnp.float32
    )
    packed, taken = tiles_out.shape[1:]
    slots = examples // packed
    slot_width = taken // slots
    slot = lax.broadcasted_iota(jnp.int32, (examples, taken), 1) // slot_width
    for position in range(shard_count):
        band = products[position * wide:(position + 1) * wide]
        start = (position + STEPS[0]) * wide % total
        band = pltpu.roll(band, (total - start) % total, 1)[:, :taken]
        for number in range(domain_count):
            tile = band[number * examples:(number + 1) * examples]
            line = tile
            for index in range(1, slots):
                moved = pltpu.roll(tile, examples - index * packed, 0)
                moved = pltpu.roll(moved, index * slot_width, 1)
                line = jnp.where(slot == index, moved, line)
            tiles_out[position * domain_count + number] = line[:packed]


def kernel(domain_count, shard_count, owners, grads, pairs_in, out, own, pairs, rows_in,
           tiles_out, tiles_in, load_sem, pairs_sem, send_sem, recv_sem, send_sem2, recv_sem2):
    devices = domain_count * shard_count
    domain, shard = lax.axis_index("domain"), lax.axis_index("shard")
    here = shard * domain_count + domain
    examples, full_width = own.shape
    width = full_width // owners
    owner = here < owners

    def place(index):
        return {"domain": index % domain_count, "shard": index // domain_count}

    def rows_copy(source, target):
        return pltpu.make_async_remote_copy(
            src_ref=own.at[:, pl.ds(target * width, width)],
            dst_ref=rows_in.at[source],
            send_sem=send_sem.at[target],
            recv_sem=recv_sem.at[source],
            device_id=place(target),
            device_id_type=pl.DeviceIdType.MESH,
        )

    def tile_copy(source, target):
        return pltpu.make_async_remote_copy(
            src_ref=tiles_out.at[target],
            dst_ref=tiles_in.at[source],
            send_sem=send_sem2.at[target],
            recv_sem=recv_sem2.at[source],
            device_id=place(target),
            device_id_type=pl.DeviceIdType.MESH,
        )

    def for_others(count, act):
        for index in range(count):
            @pl.when(index != here)
            def _():
                act(index)

    load = pltpu.make_async_copy(grads, own, load_sem)
    load.start()
    counts = pltpu.make_async_copy(pairs_in, pairs, pairs_sem)
    counts.start()
    barrier = pltpu.get_barrier_semaphore()

    @pl.when(owner)
    def _():
        for_others(devices, lambda index: pl.semaphore_signal(
            barrier, inc=1, device_id=place(index), device_id_type=pl.DeviceIdType.MESH
        ))

    load.wait()

    @pl.when(owner)
    def _():
        mine = pl.ds(pl.multiple_of(here * width, LANES), width)
        rows_in[pl.ds(here, 1)] = own[:, mine][None]
        pl.semaphore_wait(barrier, owners - 1)

    if owners < devices:
        @pl.when(jnp.logical_not(owner))
        def _():
            pl.semaphore_wait(barrier, owners)

    for_others(owners, lambda index: rows_copy(here, index).start())

    @pl.when(owner)
    def _():
        for_others(devices, lambda index: rows_copy(index, 0).wait_recv())
        total = devices * examples
        rows = rows_in[...].astype(jnp.float32).reshape(total, width).astype(jnp.bfloat16)
        influence_tiles(rows, tiles_out, domain_count, shard_count, examples)
        for_others(devices, lambda index: tile_copy(here, index).start())
        tiles_in[pl.ds(here, 1)] = tiles_out[pl.ds(here, 1)]

    columns = out.shape[-1]
    counts.wait()
    column = lax.broadcasted_iota(jnp.int32, (examples, columns), 1)
    column_domain = lax.rem(lax.div(column, examples), domain_count)
    limits = jnp.zeros((examples, columns), jnp.int32)
    for number in range(domain_count):
        limit = pairs[domain, number] * (examples // COUNT_MAX)
        limits = jnp.where(column_domain == number, limit, limits)
    row = lax.broadcasted_iota(jnp.int32, (examples, columns), 0)
    kept = (row < limits) & (lax.rem(column, examples) < limits)
    for_others(owners, lambda index: tile_copy(index, 0).wait_recv())
    packed, taken = tiles_in.shape[1:]
    slots = examples // packed
    slot_width = taken // slots
    summed = jnp.sum(tiles_in[...], axis=0) * (1.0 / math.sqrt(full_width))
    for index in range(slots):
        part = slice(index * packed, (index + 1) * packed)
        lines = summed[:, index * slot_width:index * slot_width + columns]
        out[part, :] = jnp.where(kept[part], lines, 0.0)
    for_others(owners, lambda index: rows_copy(here, index).wait_send())

    @pl.when(owner)
    def _():
        for_others(devices, lambda index: tile_copy(here, index).wait_send())


def owner_count(devices, full_width):
    unit = math.lcm(LANES, BLOCK_WIDTH)
    count = devices // OWNER_SHARE
    return count if count and full_width % (count * unit) == 0 else 0


def fused(gradients, pair_blocks):
    domain_count, shard_count = lax.axis_size("domain"), lax.axis_size("shard")
    devices = domain_count * shard_count
    examples, full_width = gradients.shape[1:]
    owners = owner_count(devices, full_width)
    width = full_width // owners
    columns = len(STEPS) * domain_count * examples
    taken = pl.cdiv(columns, LANES) * LANES
    slots = 2 if 2 * columns <= taken else 1
    packed = examples // slots
    one, per_owner, per_device = (
        pltpu.SemaphoreType.DMA(shape) for shape in ((), (owners,), (devices,))
    )
    result = pl.pallas_call(
        functools.partial(kernel, domain_count, shard_count, owners),
        out_shape=jax.ShapeDtypeStruct((examples, columns), jnp.float32),
        in_specs=[
            pl.BlockSpec(memory_space=pl.ANY),
            pl.BlockSpec(memory_space=pl.ANY),
        ],
        out_specs=pl.BlockSpec(memory_space=pltpu.VMEM),
        scratch_shapes=[
            pltpu.VMEM((examples, full_width), gradients.dtype),
            pltpu.SMEM(pair_blocks.shape, pair_blocks.dtype),
            pltpu.VMEM((devices, examples, width), gradients.dtype),
            pltpu.VMEM((devices, packed, taken), jnp.float32),
            pltpu.VMEM((owners, packed, taken), jnp.float32),
            one, one, per_owner, per_device, per_device, per_owner,
        ],
        compiler_params=pltpu.CompilerParams(collective_id=0, has_side_effects=True),
        name="influence",
    )(gradients[0], pair_blocks)
    return result[None]


def shifted(value, axis, steps):
    count = lax.axis_size(axis)
    pairs = [(source, (source + steps) % count) for source in range(count)]
    return lax.ppermute(value, axis, pairs)


def invert(statistics, example_total):
    traces = jnp.einsum("bpp->b", statistics)
    order = statistics.shape[-1]
    identity = jnp.eye(order, dtype=jnp.float32)
    fisher = (
        statistics / example_total
        + (damping * traces / (order * example_total))[:, None, None] * identity
    )
    factor = jnp.linalg.cholesky(fisher)
    identities = jnp.broadcast_to(identity, fisher.shape)
    factor_inv = lax.linalg.triangular_solve(factor, identities, left_side=True, lower=True)
    return jnp.einsum("bkp,bkq->bpq", factor_inv, factor_inv, precision=lax.Precision.HIGHEST)


def local(gradients, pair_blocks):
    own_rows = gradients[0]
    examples_here, full_width = own_rows.shape
    module_count = full_width // BLOCK_WIDTH
    domain_count = lax.axis_size("domain")
    example_total = examples_here * domain_count * lax.axis_size("shard")
    blocked = own_rows.reshape(examples_here, module_count, BLOCK_WIDTH)
    statistics = jnp.einsum("ibp,ibq->bpq", blocked, blocked, preferred_element_type=jnp.float32)
    partial_sum = lax.psum_scatter(statistics, "shard", scatter_dimension=0, tiled=True)
    partial_sum = lax.psum(partial_sum, "domain")
    inverse = lax.all_gather(invert(partial_sum, example_total), "shard", axis=0, tiled=True)
    precond = jnp.einsum(
        "ibp,bpq->ibq", blocked.astype(jnp.float32), inverse, precision=lax.Precision.HIGHEST
    )
    precond = precond.reshape(examples_here, full_width).astype(jnp.bfloat16)
    inv_root = 1.0 / math.sqrt(full_width)
    domain_index = lax.axis_index("domain")
    row_pieces = []
    for step_by in (-1, 0, 1):
        if step_by == 0:
            row_pieces.append(precond)
        else:
            row_pieces.append(shifted(precond, "shard", step_by))
    queries = jnp.concatenate(row_pieces, 0)
    wide = domain_count * examples_here
    direct = (
        jnp.einsum(
            "ik,jk->ij",
            queries,
            lax.all_gather(own_rows, "domain", axis=0, tiled=True),
            preferred_element_type=jnp.float32,
        )
        * inv_root
    )
    row_blocks = direct.reshape(3, examples_here, wide)
    received = []
    for step_by in (-1, 0, 1):
        if step_by == 0:
            received.append(row_blocks[1])
        else:
            received.append(shifted(row_blocks[step_by + 1], "shard", -step_by))
    final = jnp.stack(received, 0)
    raw_tiles = jnp.transpose(final, (1, 0, 2)).reshape(examples_here, 3 * wide)
    counts = lax.dynamic_index_in_dim(pair_blocks, domain_index, 0, keepdims=False)
    column_all = jnp.arange(3 * wide, dtype=jnp.int32)
    column_domain = column_all // examples_here % domain_count
    limits = jnp.take(counts * (examples_here // COUNT_MAX), column_domain)
    column_index = column_all % examples_here
    row_index = jnp.arange(examples_here, dtype=jnp.int32)
    kept_mask = (row_index[:, None] < limits[None, :]) & (column_index < limits)[None, :]
    return jnp.where(kept_mask, raw_tiles, 0.0)[None]


def solution(mesh):
    placed = (P("domain", "shard", None), P())

    def body(gradients, pair_blocks):
        domain_count, shard_count = mesh.shape["domain"], mesh.shape["shard"]
        devices = domain_count * shard_count
        examples, full_width = gradients.shape[1:]
        columns = len(STEPS) * domain_count * examples
        if owner_count(devices, full_width) and examples % 8 == 0 and columns <= devices * examples:
            return fused(gradients, pair_blocks)
        return local(gradients, pair_blocks)

    return jax.shard_map(
        body, mesh=mesh, in_specs=placed, out_specs=P("domain", "shard", None), check_vma=False
    )
```

```python
import functools
import math

import jax
import jax.numpy as jnp
from jax import lax
from jax.experimental import pallas as pl
from jax.experimental.pallas import tpu as pltpu
from jax.sharding import PartitionSpec as P

BLOCK_WIDTH = 64
COUNT_MAX = 4
LANES = 128
STEPS = (-1, 0, 1)
OWNER_SHARE = 2


damping = 0.5


def split(value):
    high = value.astype(jnp.bfloat16)
    rest = value - high.astype(jnp.float32)
    middle = rest.astype(jnp.bfloat16)
    low = (rest - middle.astype(jnp.float32)).astype(jnp.bfloat16)
    return high, middle, low


def beside(*parts):
    return jnp.concatenate(parts, axis=1)


def above(*parts):
    return jnp.concatenate(parts, axis=0)


def wide_dot(left, right):
    return jnp.dot(left, right, preferred_element_type=jnp.float32)


def short_dot(left, right):
    width = right.shape[1]
    left_high, left_middle, _ = split(left)
    right_high, right_middle, _ = split(right)
    weights = above(
        beside(right_high, right_middle), beside(right_high, jnp.zeros_like(right_middle))
    )
    both = wide_dot(beside(left_high, left_middle), weights)
    return both[:, :width] + both[:, width:]


def exact_dot(left, right):
    width = right.shape[1]
    left_high, left_middle, left_low = split(left)
    right_high, right_middle, right_low = split(right)
    line = beside(right_high, right_middle)
    both = wide_dot(beside(left_high, left_middle), above(line, line))
    small = wide_dot(beside(left_high, left_low), above(right_low, right_high))
    return both[:, :width] + (both[:, width:] + small)


def invert_modules(groups, example_total):
    order = BLOCK_WIDTH
    width = groups[0].shape[0]
    row = lax.broadcasted_iota(jnp.int32, (width, width), 0)
    column = lax.broadcasted_iota(jnp.int32, (width, width), 1)
    same = row // order == column // order
    diagonal = row == column
    identity = jnp.where(diagonal, 1.0, 0.0)
    lane = lax.broadcasted_iota(jnp.int32, (1, width), 1) // order
    low, high = damping, order + damping
    bound = (high + low) / (high - low)
    scales, scaled, inverses, residuals = [], [], [], []
    now, later = bound, 2.0 * bound * bound - 1.0
    gain = 2.0 * now * now / later
    for statistics in groups:
        entries = jnp.sum(jnp.where(diagonal, statistics, 0.0), axis=0, keepdims=True)
        traces = jnp.zeros((1, width), jnp.float32)
        for module in range(width // order):
            here = lane == module
            total = jnp.sum(jnp.where(here, entries, 0.0), axis=1, keepdims=True)
            traces = jnp.where(here, total, traces)
        scale = order / traces
        matrix = jnp.where(same, statistics * scale, 0.0) + damping * identity
        residual = identity - (2.0 / (high + low)) * matrix
        scales.append(scale)
        scaled.append(matrix)
        inverses.append((gain * 2.0 / (high + low)) * (identity + residual))
        residuals.append(residual)
    products = [short_dot(residual, residual) for residual in residuals]
    residuals = [gain * product - (1.0 / later) * identity for product in products]
    while later < 1e4:
        now, later = later, 2.0 * later * later - 1.0
        gain = 2.0 * now * now / later
        products = [
            short_dot(above(inverse, residual), residual)
            for inverse, residual in zip(inverses, residuals)
        ]
        inverses = [
            gain * (inverse + both[:width]) for inverse, both in zip(inverses, products)
        ]
        residuals = [gain * both[width:] - (1.0 / later) * identity for both in products]
    errors = [
        identity - exact_dot(matrix, inverse) for matrix, inverse in zip(scaled, inverses)
    ]
    products = [short_dot(inverse, error) for inverse, error in zip(inverses, errors)]
    return [
        (inverse + product) * (scale * example_total)
        for inverse, product, scale in zip(inverses, products, scales)
    ]


def influence_tiles(rows, tiles_out, domain_count, shard_count, examples):
    total, width = rows.shape
    wide = domain_count * examples
    statistics = lax.dot_general(
        rows, rows, (((0,), (0,)), ((), ())), preferred_element_type=jnp.float32
    )
    spans = [slice(start, start + LANES) for start in range(0, width, LANES)]
    inverses = invert_modules([statistics[span, span] for span in spans], float(total))
    pieces = []
    for span, inverse in zip(spans, inverses):
        high, middle, low = split(inverse)
        group = rows[:, span]
        piece = wide_dot(beside(group, group), above(high, middle)) + wide_dot(group, low)
        pieces.append(piece.astype(jnp.bfloat16))
    products = lax.dot_general(
        beside(*pieces), rows, (((1,), (1,)), ((), ())), preferred_element_type=jnp.float32
    )
    packed, taken = tiles_out.shape[1:]
    slots = examples // packed
    slot_width = taken // slots
    slot = lax.broadcasted_iota(jnp.int32, (examples, taken), 1) // slot_width
    for position in range(shard_count):
        band = products[position * wide:(position + 1) * wide]
        start = (position + STEPS[0]) * wide % total
        band = pltpu.roll(band, (total - start) % total, 1)[:, :taken]
        for number in range(domain_count):
            tile = band[number * examples:(number + 1) * examples]
            line = tile
            for index in range(1, slots):
                moved = pltpu.roll(tile, examples - index * packed, 0)
                moved = pltpu.roll(moved, index * slot_width, 1)
                line = jnp.where(slot == index, moved, line)
            tiles_out[position * domain_count + number] = line[:packed]


def kernel(domain_count, shard_count, owners, grads, pairs_in, out, own, pairs, rows_in,
           tiles_out, tiles_in, load_sem, pairs_sem, send_sem, recv_sem, send_sem2, recv_sem2):
    devices = domain_count * shard_count
    domain, shard = lax.axis_index("domain"), lax.axis_index("shard")
    here = shard * domain_count + domain
    examples, full_width = own.shape
    width = full_width // owners
    owner = here < owners

    def place(index):
        return {"domain": index % domain_count, "shard": index // domain_count}

    def rows_copy(source, target):
        return pltpu.make_async_remote_copy(
            src_ref=own.at[:, pl.ds(target * width, width)],
            dst_ref=rows_in.at[source],
            send_sem=send_sem,
            recv_sem=recv_sem,
            device_id=place(target),
            device_id_type=pl.DeviceIdType.MESH,
        )

    def tile_copy(source, target):
        return pltpu.make_async_remote_copy(
            src_ref=tiles_out.at[target],
            dst_ref=tiles_in.at[source],
            send_sem=send_sem2,
            recv_sem=recv_sem2,
            device_id=place(target),
            device_id_type=pl.DeviceIdType.MESH,
        )

    def for_others(count, act):
        for index in range(count):
            @pl.when(index != here)
            def _():
                act(index)

    def wait_for(blocks, count, semaphore):
        several = blocks.at[pl.ds(0, count)]
        pltpu.make_async_copy(several, several, semaphore).wait()

    def wait_for_owners(blocks, semaphore):
        @pl.when(owner)
        def _():
            wait_for(blocks, owners - 1, semaphore)

        if owners < devices:
            @pl.when(jnp.logical_not(owner))
            def _():
                wait_for(blocks, owners, semaphore)

    load = pltpu.make_async_copy(grads, own, load_sem)
    load.start()
    counts = pltpu.make_async_copy(pairs_in, pairs, pairs_sem)
    counts.start()
    barrier = pltpu.get_barrier_semaphore()

    @pl.when(owner)
    def _():
        for_others(devices, lambda index: pl.semaphore_signal(
            barrier, inc=1, device_id=place(index), device_id_type=pl.DeviceIdType.MESH
        ))

    load.wait()

    @pl.when(owner)
    def _():
        mine = pl.ds(pl.multiple_of(here * width, LANES), width)
        rows_in[pl.ds(here, 1)] = own[:, mine][None]
        pl.semaphore_wait(barrier, owners - 1)

    if owners < devices:
        @pl.when(jnp.logical_not(owner))
        def _():
            pl.semaphore_wait(barrier, owners)

    for_others(owners, lambda index: rows_copy(here, index).start())

    @pl.when(owner)
    def _():
        wait_for(rows_in, devices - 1, recv_sem)
        total = devices * examples
        rows = rows_in[...].astype(jnp.float32).reshape(total, width).astype(jnp.bfloat16)
        influence_tiles(rows, tiles_out, domain_count, shard_count, examples)
        for_others(devices, lambda index: tile_copy(here, index).start())
        tiles_in[pl.ds(here, 1)] = tiles_out[pl.ds(here, 1)]

    columns = out.shape[-1]
    counts.wait()
    column = lax.broadcasted_iota(jnp.int32, (examples, columns), 1)
    column_domain = lax.rem(lax.div(column, examples), domain_count)
    limits = jnp.zeros((examples, columns), jnp.int32)
    for number in range(domain_count):
        limit = pairs[domain, number] * (examples // COUNT_MAX)
        limits = jnp.where(column_domain == number, limit, limits)
    row = lax.broadcasted_iota(jnp.int32, (examples, columns), 0)
    kept = (row < limits) & (lax.rem(column, examples) < limits)
    wait_for_owners(rows_in, send_sem)
    wait_for_owners(tiles_in, recv_sem2)
    packed, taken = tiles_in.shape[1:]
    slots = examples // packed
    slot_width = taken // slots
    summed = jnp.sum(tiles_in[...], axis=0) * (1.0 / math.sqrt(full_width))
    for index in range(slots):
        part = slice(index * packed, (index + 1) * packed)
        lines = summed[:, index * slot_width:index * slot_width + columns]
        out[part, :] = jnp.where(kept[part], lines, 0.0)

    @pl.when(owner)
    def _():
        wait_for(tiles_out, devices - 1, send_sem2)


def owner_count(devices, full_width):
    unit = math.lcm(LANES, BLOCK_WIDTH)
    count = devices // OWNER_SHARE
    return count if count and full_width % (count * unit) == 0 else 0


def fused(gradients, pair_blocks):
    domain_count, shard_count = lax.axis_size("domain"), lax.axis_size("shard")
    devices = domain_count * shard_count
    examples, full_width = gradients.shape[1:]
    owners = owner_count(devices, full_width)
    width = full_width // owners
    columns = len(STEPS) * domain_count * examples
    taken = pl.cdiv(columns, LANES) * LANES
    slots = 2 if 2 * columns <= taken else 1
    packed = examples // slots
    result = pl.pallas_call(
        functools.partial(kernel, domain_count, shard_count, owners),
        out_shape=pltpu.VMEM((examples, columns), jnp.float32),
        in_specs=[
            pl.BlockSpec(memory_space=pl.ANY),
            pl.BlockSpec(memory_space=pl.ANY),
        ],
        out_specs=pl.BlockSpec(memory_space=pltpu.VMEM),
        scratch_shapes=[
            pltpu.VMEM((examples, full_width), gradients.dtype),
            pltpu.SMEM(pair_blocks.shape, pair_blocks.dtype),
            pltpu.VMEM((devices, examples, width), gradients.dtype),
            pltpu.VMEM((devices, packed, taken), jnp.float32),
            pltpu.VMEM((owners, packed, taken), jnp.float32),
            *[pltpu.SemaphoreType.DMA] * 6,
        ],
        compiler_params=pltpu.CompilerParams(collective_id=0, has_side_effects=True),
        name="influence",
    )(gradients[0], pair_blocks)
    return result[None]


def shifted(value, axis, steps):
    count = lax.axis_size(axis)
    pairs = [(source, (source + steps) % count) for source in range(count)]
    return lax.ppermute(value, axis, pairs)


def invert(statistics, example_total):
    traces = jnp.einsum("bpp->b", statistics)
    order = statistics.shape[-1]
    identity = jnp.eye(order, dtype=jnp.float32)
    fisher = (
        statistics / example_total
        + (damping * traces / (order * example_total))[:, None, None] * identity
    )
    factor = jnp.linalg.cholesky(fisher)
    identities = jnp.broadcast_to(identity, fisher.shape)
    factor_inv = lax.linalg.triangular_solve(factor, identities, left_side=True, lower=True)
    return jnp.einsum("bkp,bkq->bpq", factor_inv, factor_inv, precision=lax.Precision.HIGHEST)


def local(gradients, pair_blocks):
    own_rows = gradients[0]
    examples_here, full_width = own_rows.shape
    module_count = full_width // BLOCK_WIDTH
    domain_count = lax.axis_size("domain")
    example_total = examples_here * domain_count * lax.axis_size("shard")
    blocked = own_rows.reshape(examples_here, module_count, BLOCK_WIDTH)
    statistics = jnp.einsum("ibp,ibq->bpq", blocked, blocked, preferred_element_type=jnp.float32)
    partial_sum = lax.psum_scatter(statistics, "shard", scatter_dimension=0, tiled=True)
    partial_sum = lax.psum(partial_sum, "domain")
    inverse = lax.all_gather(invert(partial_sum, example_total), "shard", axis=0, tiled=True)
    precond = jnp.einsum(
        "ibp,bpq->ibq", blocked.astype(jnp.float32), inverse, precision=lax.Precision.HIGHEST
    )
    precond = precond.reshape(examples_here, full_width).astype(jnp.bfloat16)
    inv_root = 1.0 / math.sqrt(full_width)
    domain_index = lax.axis_index("domain")
    row_pieces = []
    for step_by in (-1, 0, 1):
        if step_by == 0:
            row_pieces.append(precond)
        else:
            row_pieces.append(shifted(precond, "shard", step_by))
    queries = jnp.concatenate(row_pieces, 0)
    wide = domain_count * examples_here
    direct = (
        jnp.einsum(
            "ik,jk->ij",
            queries,
            lax.all_gather(own_rows, "domain", axis=0, tiled=True),
            preferred_element_type=jnp.float32,
        )
        * inv_root
    )
    row_blocks = direct.reshape(3, examples_here, wide)
    received = []
    for step_by in (-1, 0, 1):
        if step_by == 0:
            received.append(row_blocks[1])
        else:
            received.append(shifted(row_blocks[step_by + 1], "shard", -step_by))
    final = jnp.stack(received, 0)
    raw_tiles = jnp.transpose(final, (1, 0, 2)).reshape(examples_here, 3 * wide)
    counts = lax.dynamic_index_in_dim(pair_blocks, domain_index, 0, keepdims=False)
    column_all = jnp.arange(3 * wide, dtype=jnp.int32)
    column_domain = column_all // examples_here % domain_count
    limits = jnp.take(counts * (examples_here // COUNT_MAX), column_domain)
    column_index = column_all % examples_here
    row_index = jnp.arange(examples_here, dtype=jnp.int32)
    kept_mask = (row_index[:, None] < limits[None, :]) & (column_index < limits)[None, :]
    return jnp.where(kept_mask, raw_tiles, 0.0)[None]


def solution(mesh):
    placed = (P("domain", "shard", None), P())

    def body(gradients, pair_blocks):
        domain_count, shard_count = mesh.shape["domain"], mesh.shape["shard"]
        devices = domain_count * shard_count
        examples, full_width = gradients.shape[1:]
        columns = len(STEPS) * domain_count * examples
        if owner_count(devices, full_width) and examples % 8 == 0 and columns <= devices * examples:
            return fused(gradients, pair_blocks)
        return local(gradients, pair_blocks)

    return jax.shard_map(
        body, mesh=mesh, in_specs=placed, out_specs=P("domain", "shard", None), check_vma=False
    )
```

```python
import functools
import math

import jax
import jax.numpy as jnp
from jax import lax
from jax.experimental import pallas as pl
from jax.experimental.pallas import tpu as pltpu
from jax.sharding import PartitionSpec as P

BLOCK_WIDTH = 64
COUNT_MAX = 4
LANES = 128
STEPS = (-1, 0, 1)
OWNER_SHARE = 4


damping = 0.5


def split(value):
    high = value.astype(jnp.bfloat16)
    rest = value - high.astype(jnp.float32)
    middle = rest.astype(jnp.bfloat16)
    low = (rest - middle.astype(jnp.float32)).astype(jnp.bfloat16)
    return high, middle, low


def beside(*parts):
    return jnp.concatenate(parts, axis=1)


def above(*parts):
    return jnp.concatenate(parts, axis=0)


def wide_dot(left, right):
    return jnp.dot(left, right, preferred_element_type=jnp.float32)


def short_dot(lefts, right):
    width = right.shape[1]
    right_high, right_middle, _ = split(right)
    parts = [
        (right_high, right_middle) if left is right else split(left)[:2] for left in lefts
    ]
    weights = above(
        beside(right_high, right_middle), beside(right_high, jnp.zeros_like(right_middle))
    )
    both = wide_dot(above(*[beside(*part) for part in parts]), weights)
    return both[:, :width] + both[:, width:]


def exact_dot(left, right):
    width = right.shape[1]
    left_high, left_middle, left_low = split(left)
    right_high, right_middle, right_low = split(right)
    line = beside(right_high, right_middle)
    both = wide_dot(beside(left_high, left_middle), above(line, line))
    small = wide_dot(beside(left_high, left_low), above(right_low, right_high))
    return both[:, :width] + (both[:, width:] + small)


def invert_modules(groups, example_total):
    order = BLOCK_WIDTH
    width = groups[0].shape[0]
    row = lax.broadcasted_iota(jnp.int32, (width, width), 0)
    column = lax.broadcasted_iota(jnp.int32, (width, width), 1)
    same = row // order == column // order
    diagonal = row == column
    identity = jnp.where(diagonal, 1.0, 0.0)
    lane = lax.broadcasted_iota(jnp.int32, (1, width), 1) // order
    low, high = damping, order + damping
    bound = (high + low) / (high - low)
    scales, scaled, inverses, residuals = [], [], [], []
    now, later = bound, 2.0 * bound * bound - 1.0
    gain = 2.0 * now * now / later
    for statistics in groups:
        entries = jnp.sum(jnp.where(diagonal, statistics, 0.0), axis=0, keepdims=True)
        traces = jnp.zeros((1, width), jnp.float32)
        for module in range(width // order):
            here = lane == module
            total = jnp.sum(jnp.where(here, entries, 0.0), axis=1, keepdims=True)
            traces = jnp.where(here, total, traces)
        scale = order / traces
        matrix = jnp.where(same, statistics * scale, 0.0) + damping * identity
        residual = identity - (2.0 / (high + low)) * matrix
        scales.append(scale)
        scaled.append(matrix)
        inverses.append((gain * 2.0 / (high + low)) * (identity + residual))
        residuals.append(residual)
    products = [short_dot([residual], residual) for residual in residuals]
    residuals = [gain * product - (1.0 / later) * identity for product in products]
    while later < 1e4:
        now, later = later, 2.0 * later * later - 1.0
        gain = 2.0 * now * now / later
        products = [
            short_dot([inverse, residual] if later < 1e4 else [inverse], residual)
            for inverse, residual in zip(inverses, residuals)
        ]
        inverses = [
            gain * (inverse + both[:width]) for inverse, both in zip(inverses, products)
        ]
        if later < 1e4:
            residuals = [gain * both[width:] - (1.0 / later) * identity for both in products]
    errors = [
        identity - exact_dot(matrix, inverse) for matrix, inverse in zip(scaled, inverses)
    ]
    products = [short_dot([inverse], error) for inverse, error in zip(inverses, errors)]
    return [
        (inverse + product) * (scale * example_total)
        for inverse, product, scale in zip(inverses, products, scales)
    ]


def influence_tiles(rows, tiles_out, domain_count, shard_count, examples, send):
    total, width = rows.shape
    wide = domain_count * examples
    statistics = lax.dot_general(
        rows, rows, (((0,), (0,)), ((), ())), preferred_element_type=jnp.float32
    )
    spans = [slice(start, start + LANES) for start in range(0, width, LANES)]
    inverses = invert_modules([statistics[span, span] for span in spans], float(total))
    pieces = []
    for span, inverse in zip(spans, inverses):
        high, middle, low = split(inverse)
        group = rows[:, span]
        piece = wide_dot(beside(group, group), above(high, middle)) + wide_dot(group, low)
        pieces.append(piece.astype(jnp.bfloat16))
    products = lax.dot_general(
        beside(*pieces), rows, (((1,), (1,)), ((), ())), preferred_element_type=jnp.float32
    )
    packed, taken = tiles_out.shape[1:]
    slots = examples // packed
    slot_width = taken // slots
    slot = lax.broadcasted_iota(jnp.int32, (examples, taken), 1) // slot_width
    for position in range(shard_count):
        band = products[position * wide:(position + 1) * wide]
        start = (position + STEPS[0]) * wide % total
        band = pltpu.roll(band, (total - start) % total, 1)[:, :taken]
        for number in range(domain_count):
            tile = band[number * examples:(number + 1) * examples]
            line = tile
            for index in range(1, slots):
                moved = pltpu.roll(tile, examples - index * packed, 0)
                moved = pltpu.roll(moved, index * slot_width, 1)
                line = jnp.where(slot == index, moved, line)
            tiles_out[position * domain_count + number] = line[:packed]
        if position in (0, shard_count - 1):
            send(range(0 if position == 0 else domain_count, (position + 1) * domain_count))


def kernel(domain_count, shard_count, owner_list, grads, pairs_in, out, own, pairs, rows_in,
           tiles_out, tiles_in, load_sem, pairs_sem, send_sem, recv_sem, send_sem2, recv_sem2):
    devices = domain_count * shard_count
    domain, shard = lax.axis_index("domain"), lax.axis_index("shard")
    here = shard * domain_count + domain
    examples, full_width = own.shape
    owners = len(owner_list)
    width = full_width // owners
    rank, owner = jnp.int32(0), jnp.bool_(False)
    for index, device in enumerate(owner_list):
        rank = jnp.where(here == device, index, rank)
        owner = jnp.logical_or(owner, here == device)

    def place(index):
        return {"domain": index % domain_count, "shard": index // domain_count}

    def rows_copy(target):
        return pltpu.make_async_remote_copy(
            src_ref=own.at[:, pl.ds(owner_list.index(target) * width, width)],
            dst_ref=rows_in.at[here],
            send_sem=send_sem,
            recv_sem=recv_sem,
            device_id=place(target),
            device_id_type=pl.DeviceIdType.MESH,
        )

    def tile_copy(target):
        return pltpu.make_async_remote_copy(
            src_ref=tiles_out.at[target],
            dst_ref=tiles_in.at[rank],
            send_sem=send_sem2,
            recv_sem=recv_sem2,
            device_id=place(target),
            device_id_type=pl.DeviceIdType.MESH,
        )

    def for_others(devices_of, act):
        for index in devices_of:
            @pl.when(index != here)
            def _():
                act(index)

    def wait_for(blocks, count, semaphore):
        several = blocks.at[pl.ds(0, count)]
        pltpu.make_async_copy(several, several, semaphore).wait()

    def wait_for_owners(blocks, semaphore):
        @pl.when(owner)
        def _():
            wait_for(blocks, owners - 1, semaphore)

        if owners < devices:
            @pl.when(jnp.logical_not(owner))
            def _():
                wait_for(blocks, owners, semaphore)

    load = pltpu.make_async_copy(grads, own, load_sem)
    load.start()
    counts = pltpu.make_async_copy(pairs_in, pairs, pairs_sem)
    counts.start()
    barrier = pltpu.get_barrier_semaphore()

    @pl.when(owner)
    def _():
        for_others(range(devices), lambda index: pl.semaphore_signal(
            barrier, inc=1, device_id=place(index), device_id_type=pl.DeviceIdType.MESH
        ))

    load.wait()

    @pl.when(owner)
    def _():
        mine = pl.ds(pl.multiple_of(rank * width, LANES), width)
        rows_in[pl.ds(here, 1)] = own[:, mine][None]
        pl.semaphore_wait(barrier, owners - 1)

    if owners < devices:
        @pl.when(jnp.logical_not(owner))
        def _():
            pl.semaphore_wait(barrier, owners)

    for_others(owner_list[::-1], lambda index: rows_copy(index).start())

    @pl.when(owner)
    def _():
        wait_for(rows_in, devices - 1, recv_sem)
        total = devices * examples
        rows = rows_in[...].astype(jnp.float32).reshape(total, width).astype(jnp.bfloat16)

        def send(targets):
            for_others(targets, lambda index: tile_copy(index).start())

        influence_tiles(rows, tiles_out, domain_count, shard_count, examples, send)
        tiles_in[pl.ds(rank, 1)] = tiles_out[pl.ds(here, 1)]

    columns = out.shape[-1]
    counts.wait()
    column = lax.broadcasted_iota(jnp.int32, (examples, columns), 1)
    column_domain = lax.rem(lax.div(column, examples), domain_count)
    limits = jnp.zeros((examples, columns), jnp.int32)
    for number in range(domain_count):
        limit = pairs[domain, number] * (examples // COUNT_MAX)
        limits = jnp.where(column_domain == number, limit, limits)
    row = lax.broadcasted_iota(jnp.int32, (examples, columns), 0)
    kept = (row < limits) & (lax.rem(column, examples) < limits)
    wait_for_owners(rows_in, send_sem)
    wait_for_owners(tiles_in, recv_sem2)
    packed, taken = tiles_in.shape[1:]
    slots = examples // packed
    slot_width = taken // slots
    summed = jnp.sum(tiles_in[...], axis=0) * (1.0 / math.sqrt(full_width))
    for index in range(slots):
        part = slice(index * packed, (index + 1) * packed)
        lines = summed[:, index * slot_width:index * slot_width + columns]
        out[part, :] = jnp.where(kept[part], lines, 0.0)

    @pl.when(owner)
    def _():
        wait_for(tiles_out, devices - 1, send_sem2)


def choose_owners(mesh, full_width):
    domain_count, shard_count = mesh.shape["domain"], mesh.shape["shard"]
    devices = domain_count * shard_count
    count = devices // OWNER_SHARE
    if not count or full_width % (count * math.lcm(LANES, BLOCK_WIDTH)):
        return []
    flat = [mesh.devices[index % domain_count, index // domain_count] for index in range(devices)]
    places = [getattr(device, "coords", None) or () for device in flat]

    def hops(index):
        return sum(abs(a - b) for a, b in zip(places[index], places[0]))

    return sorted(range(devices), key=lambda index: (hops(index), index))[:count]


def fused(gradients, pair_blocks, owner_list):
    domain_count, shard_count = lax.axis_size("domain"), lax.axis_size("shard")
    devices = domain_count * shard_count
    examples, full_width = gradients.shape[1:]
    owners = len(owner_list)
    width = full_width // owners
    columns = len(STEPS) * domain_count * examples
    taken = pl.cdiv(columns, LANES) * LANES
    slots = 2 if 2 * columns <= taken else 1
    packed = examples // slots
    result = pl.pallas_call(
        functools.partial(kernel, domain_count, shard_count, owner_list),
        out_shape=pltpu.VMEM((examples, columns), jnp.float32),
        in_specs=[
            pl.BlockSpec(memory_space=pl.ANY),
            pl.BlockSpec(memory_space=pl.ANY),
        ],
        out_specs=pl.BlockSpec(memory_space=pltpu.VMEM),
        scratch_shapes=[
            pltpu.VMEM((examples, full_width), gradients.dtype),
            pltpu.SMEM(pair_blocks.shape, pair_blocks.dtype),
            pltpu.VMEM((devices, examples, width), gradients.dtype),
            pltpu.VMEM((devices, packed, taken), jnp.float32),
            pltpu.VMEM((owners, packed, taken), jnp.float32),
            *[pltpu.SemaphoreType.DMA] * 6,
        ],
        compiler_params=pltpu.CompilerParams(collective_id=0, has_side_effects=True),
        name="influence",
    )(gradients[0], pair_blocks)
    return result[None]


def shifted(value, axis, steps):
    count = lax.axis_size(axis)
    pairs = [(source, (source + steps) % count) for source in range(count)]
    return lax.ppermute(value, axis, pairs)


def invert(statistics, example_total):
    traces = jnp.einsum("bpp->b", statistics)
    order = statistics.shape[-1]
    identity = jnp.eye(order, dtype=jnp.float32)
    fisher = (
        statistics / example_total
        + (damping * traces / (order * example_total))[:, None, None] * identity
    )
    factor = jnp.linalg.cholesky(fisher)
    identities = jnp.broadcast_to(identity, fisher.shape)
    factor_inv = lax.linalg.triangular_solve(factor, identities, left_side=True, lower=True)
    return jnp.einsum("bkp,bkq->bpq", factor_inv, factor_inv, precision=lax.Precision.HIGHEST)


def local(gradients, pair_blocks):
    own_rows = gradients[0]
    examples_here, full_width = own_rows.shape
    module_count = full_width // BLOCK_WIDTH
    domain_count = lax.axis_size("domain")
    example_total = examples_here * domain_count * lax.axis_size("shard")
    blocked = own_rows.reshape(examples_here, module_count, BLOCK_WIDTH)
    statistics = jnp.einsum("ibp,ibq->bpq", blocked, blocked, preferred_element_type=jnp.float32)
    partial_sum = lax.psum_scatter(statistics, "shard", scatter_dimension=0, tiled=True)
    partial_sum = lax.psum(partial_sum, "domain")
    inverse = lax.all_gather(invert(partial_sum, example_total), "shard", axis=0, tiled=True)
    precond = jnp.einsum(
        "ibp,bpq->ibq", blocked.astype(jnp.float32), inverse, precision=lax.Precision.HIGHEST
    )
    precond = precond.reshape(examples_here, full_width).astype(jnp.bfloat16)
    inv_root = 1.0 / math.sqrt(full_width)
    domain_index = lax.axis_index("domain")
    row_pieces = []
    for step_by in (-1, 0, 1):
        if step_by == 0:
            row_pieces.append(precond)
        else:
            row_pieces.append(shifted(precond, "shard", step_by))
    queries = jnp.concatenate(row_pieces, 0)
    wide = domain_count * examples_here
    direct = (
        jnp.einsum(
            "ik,jk->ij",
            queries,
            lax.all_gather(own_rows, "domain", axis=0, tiled=True),
            preferred_element_type=jnp.float32,
        )
        * inv_root
    )
    row_blocks = direct.reshape(3, examples_here, wide)
    received = []
    for step_by in (-1, 0, 1):
        if step_by == 0:
            received.append(row_blocks[1])
        else:
            received.append(shifted(row_blocks[step_by + 1], "shard", -step_by))
    final = jnp.stack(received, 0)
    raw_tiles = jnp.transpose(final, (1, 0, 2)).reshape(examples_here, 3 * wide)
    counts = lax.dynamic_index_in_dim(pair_blocks, domain_index, 0, keepdims=False)
    column_all = jnp.arange(3 * wide, dtype=jnp.int32)
    column_domain = column_all // examples_here % domain_count
    limits = jnp.take(counts * (examples_here // COUNT_MAX), column_domain)
    column_index = column_all % examples_here
    row_index = jnp.arange(examples_here, dtype=jnp.int32)
    kept_mask = (row_index[:, None] < limits[None, :]) & (column_index < limits)[None, :]
    return jnp.where(kept_mask, raw_tiles, 0.0)[None]


def solution(mesh):
    placed = (P("domain", "shard", None), P())

    def body(gradients, pair_blocks):
        domain_count, shard_count = mesh.shape["domain"], mesh.shape["shard"]
        devices = domain_count * shard_count
        examples, full_width = gradients.shape[1:]
        columns = len(STEPS) * domain_count * examples
        owner_list = choose_owners(mesh, full_width)
        if owner_list and examples % 8 == 0 and columns <= devices * examples:
            return fused(gradients, pair_blocks, owner_list)
        return local(gradients, pair_blocks)

    return jax.shard_map(
        body, mesh=mesh, in_specs=placed, out_specs=P("domain", "shard", None), check_vma=False
    )
```

```python
import functools
import math

import jax
import jax.numpy as jnp
from jax import lax
from jax.experimental import pallas as pl
from jax.experimental.pallas import tpu as pltpu
from jax.sharding import PartitionSpec as P

BLOCK_WIDTH = 64
COUNT_MAX = 4
LANES = 128
STEPS = (-1, 0, 1)
OWNER_SHARE = 4


damping = 0.5


def split(value):
    high = value.astype(jnp.bfloat16)
    rest = value - high.astype(jnp.float32)
    middle = rest.astype(jnp.bfloat16)
    low = (rest - middle.astype(jnp.float32)).astype(jnp.bfloat16)
    return high, middle, low


def beside(*parts):
    return jnp.concatenate(parts, axis=1)


def above(*parts):
    return jnp.concatenate(parts, axis=0)


def wide_dot(left, right):
    return jnp.dot(left, right, preferred_element_type=jnp.float32)


def short_dot(lefts, right):
    width = right.shape[1]
    right_high, right_middle, _ = split(right)
    parts = [
        (right_high, right_middle) if left is right else split(left)[:2] for left in lefts
    ]
    weights = above(
        beside(right_high, right_middle), beside(right_high, jnp.zeros_like(right_middle))
    )
    both = wide_dot(above(*[beside(*part) for part in parts]), weights)
    return both[:, :width] + both[:, width:]


def exact_dot(left, right):
    width = right.shape[1]
    left_high, left_middle, left_low = split(left)
    right_high, right_middle, right_low = split(right)
    line = beside(right_high, right_middle)
    both = wide_dot(beside(left_high, left_middle), above(line, line))
    small = wide_dot(beside(left_high, left_low), above(right_low, right_high))
    return both[:, :width] + (both[:, width:] + small)


def invert_modules(groups, example_total):
    order = BLOCK_WIDTH
    width = groups[0].shape[0]
    row = lax.broadcasted_iota(jnp.int32, (width, width), 0)
    column = lax.broadcasted_iota(jnp.int32, (width, width), 1)
    same = row // order == column // order
    diagonal = row == column
    identity = jnp.where(diagonal, 1.0, 0.0)
    lane = lax.broadcasted_iota(jnp.int32, (1, width), 1) // order
    low, high = damping, order + damping
    bound = (high + low) / (high - low)
    scales, scaled, inverses, residuals = [], [], [], []
    now, later = bound, 2.0 * bound * bound - 1.0
    gain = 2.0 * now * now / later
    for statistics in groups:
        entries = jnp.sum(jnp.where(diagonal, statistics, 0.0), axis=0, keepdims=True)
        traces = jnp.zeros((1, width), jnp.float32)
        for module in range(width // order):
            here = lane == module
            total = jnp.sum(jnp.where(here, entries, 0.0), axis=1, keepdims=True)
            traces = jnp.where(here, total, traces)
        scale = order / traces
        matrix = jnp.where(same, statistics * scale, 0.0) + damping * identity
        residual = identity - (2.0 / (high + low)) * matrix
        scales.append(scale)
        scaled.append(matrix)
        inverses.append((gain * 2.0 / (high + low)) * (identity + residual))
        residuals.append(residual)
    products = [short_dot([residual], residual) for residual in residuals]
    residuals = [gain * product - (1.0 / later) * identity for product in products]
    while later < 1e4:
        now, later = later, 2.0 * later * later - 1.0
        gain = 2.0 * now * now / later
        products = [
            short_dot([inverse, residual] if later < 1e4 else [inverse], residual)
            for inverse, residual in zip(inverses, residuals)
        ]
        inverses = [
            gain * (inverse + both[:width]) for inverse, both in zip(inverses, products)
        ]
        if later < 1e4:
            residuals = [gain * both[width:] - (1.0 / later) * identity for both in products]
    errors = [
        identity - exact_dot(matrix, inverse) for matrix, inverse in zip(scaled, inverses)
    ]
    products = [short_dot([inverse], error) for inverse, error in zip(inverses, errors)]
    return [
        (inverse + product) * (scale * example_total)
        for inverse, product, scale in zip(inverses, products, scales)
    ]


def influence_tiles(rows, tiles_out, domain_count, shard_count, examples, send):
    total, width = rows.shape
    wide = domain_count * examples
    spans = [slice(start, start + LANES) for start in range(0, width, LANES)]
    statistics = [
        lax.dot_general(
            rows[:, span], rows[:, span], (((0,), (0,)), ((), ())),
            preferred_element_type=jnp.float32,
        )
        for span in spans
    ]
    inverses = invert_modules(statistics, float(total))
    pieces = []
    for span, inverse in zip(spans, inverses):
        high, middle, low = split(inverse)
        group = rows[:, span]
        piece = wide_dot(beside(group, group), above(high, middle)) + wide_dot(group, low)
        pieces.append(piece.astype(jnp.bfloat16))
    products = lax.dot_general(
        beside(*pieces), rows, (((1,), (1,)), ((), ())), preferred_element_type=jnp.float32
    )
    packed, taken = tiles_out.shape[1:]
    slots = examples // packed
    slot_width = taken // slots
    slot = lax.broadcasted_iota(jnp.int32, (examples, taken), 1) // slot_width
    for position in range(shard_count):
        band = products[position * wide:(position + 1) * wide]
        start = (position + STEPS[0]) * wide % total
        band = pltpu.roll(band, (total - start) % total, 1)[:, :taken]
        for number in range(domain_count):
            tile = band[number * examples:(number + 1) * examples]
            line = tile
            for index in range(1, slots):
                moved = pltpu.roll(tile, examples - index * packed, 0)
                moved = pltpu.roll(moved, index * slot_width, 1)
                line = jnp.where(slot == index, moved, line)
            tiles_out[position * domain_count + number] = line[:packed]
        if position in (0, shard_count - 1):
            send(range(0 if position == 0 else domain_count, (position + 1) * domain_count))


def kernel(domain_count, shard_count, owner_list, grads, pairs_in, out, own, pairs, rows_in,
           tiles_out, tiles_in, load_sem, pairs_sem, send_sem, recv_sem, send_sem2, recv_sem2):
    devices = domain_count * shard_count
    domain, shard = lax.axis_index("domain"), lax.axis_index("shard")
    here = shard * domain_count + domain
    examples, full_width = own.shape
    owners = len(owner_list)
    width = full_width // owners
    rank, owner = jnp.int32(0), jnp.bool_(False)
    for index, device in enumerate(owner_list):
        rank = jnp.where(here == device, index, rank)
        owner = jnp.logical_or(owner, here == device)

    def place(index):
        return {"domain": index % domain_count, "shard": index // domain_count}

    def rows_copy(target):
        return pltpu.make_async_remote_copy(
            src_ref=own.at[:, pl.ds(owner_list.index(target) * width, width)],
            dst_ref=rows_in.at[here],
            send_sem=send_sem,
            recv_sem=recv_sem,
            device_id=place(target),
            device_id_type=pl.DeviceIdType.MESH,
        )

    def tile_copy(target):
        return pltpu.make_async_remote_copy(
            src_ref=tiles_out.at[target],
            dst_ref=tiles_in.at[rank],
            send_sem=send_sem2,
            recv_sem=recv_sem2,
            device_id=place(target),
            device_id_type=pl.DeviceIdType.MESH,
        )

    def for_others(devices_of, act):
        for index in devices_of:
            @pl.when(index != here)
            def _():
                act(index)

    def wait_for(blocks, count, semaphore):
        several = blocks.at[pl.ds(0, count)]
        pltpu.make_async_copy(several, several, semaphore).wait()

    def wait_for_owners(blocks, semaphore):
        @pl.when(owner)
        def _():
            wait_for(blocks, owners - 1, semaphore)

        if owners < devices:
            @pl.when(jnp.logical_not(owner))
            def _():
                wait_for(blocks, owners, semaphore)

    load = pltpu.make_async_copy(grads, own, load_sem)
    load.start()
    counts = pltpu.make_async_copy(pairs_in, pairs, pairs_sem)
    counts.start()
    barrier = pltpu.get_barrier_semaphore()

    @pl.when(owner)
    def _():
        for_others(range(devices), lambda index: pl.semaphore_signal(
            barrier, inc=1, device_id=place(index), device_id_type=pl.DeviceIdType.MESH
        ))

    load.wait()

    @pl.when(owner)
    def _():
        mine = pl.ds(pl.multiple_of(rank * width, LANES), width)
        rows_in[pl.ds(here, 1)] = own[:, mine][None]
        pl.semaphore_wait(barrier, owners - 1)

    if owners < devices:
        @pl.when(jnp.logical_not(owner))
        def _():
            pl.semaphore_wait(barrier, owners)

    for_others(owner_list[::-1], lambda index: rows_copy(index).start())

    @pl.when(owner)
    def _():
        wait_for(rows_in, devices - 1, recv_sem)
        total = devices * examples
        rows = rows_in[...].astype(jnp.float32).reshape(total, width).astype(jnp.bfloat16)

        def send(targets):
            for_others(targets, lambda index: tile_copy(index).start())

        influence_tiles(rows, tiles_out, domain_count, shard_count, examples, send)
        tiles_in[pl.ds(rank, 1)] = tiles_out[pl.ds(here, 1)]

    columns = out.shape[-1]
    counts.wait()
    column = lax.broadcasted_iota(jnp.int32, (examples, columns), 1)
    column_domain = lax.rem(lax.div(column, examples), domain_count)
    limits = jnp.zeros((examples, columns), jnp.int32)
    for number in range(domain_count):
        limit = pairs[domain, number] * (examples // COUNT_MAX)
        limits = jnp.where(column_domain == number, limit, limits)
    row = lax.broadcasted_iota(jnp.int32, (examples, columns), 0)
    kept = (row < limits) & (lax.rem(column, examples) < limits)
    wait_for_owners(rows_in, send_sem)
    wait_for_owners(tiles_in, recv_sem2)
    packed, taken = tiles_in.shape[1:]
    slots = examples // packed
    slot_width = taken // slots
    summed = jnp.sum(tiles_in[...], axis=0) * (1.0 / math.sqrt(full_width))
    for index in range(slots):
        part = slice(index * packed, (index + 1) * packed)
        lines = summed[:, index * slot_width:index * slot_width + columns]
        out[part, :] = jnp.where(kept[part], lines, 0.0)

    @pl.when(owner)
    def _():
        wait_for(tiles_out, devices - 1, send_sem2)


def choose_owners(mesh, full_width):
    domain_count, shard_count = mesh.shape["domain"], mesh.shape["shard"]
    devices = domain_count * shard_count
    count = devices // OWNER_SHARE
    if not count or full_width % (count * math.lcm(LANES, BLOCK_WIDTH)):
        return []
    flat = [mesh.devices[index % domain_count, index // domain_count] for index in range(devices)]
    places = [getattr(device, "coords", None) or () for device in flat]

    def hops(index):
        return sum(abs(a - b) for a, b in zip(places[index], places[0]))

    return sorted(range(devices), key=lambda index: (hops(index), index))[:count]


def fused(gradients, pair_blocks, owner_list):
    domain_count, shard_count = lax.axis_size("domain"), lax.axis_size("shard")
    devices = domain_count * shard_count
    examples, full_width = gradients.shape[1:]
    owners = len(owner_list)
    width = full_width // owners
    columns = len(STEPS) * domain_count * examples
    taken = pl.cdiv(columns, LANES) * LANES
    slots = 2 if 2 * columns <= taken else 1
    packed = examples // slots
    result = pl.pallas_call(
        functools.partial(kernel, domain_count, shard_count, owner_list),
        out_shape=pltpu.VMEM((examples, columns), jnp.float32),
        in_specs=[
            pl.BlockSpec(memory_space=pl.ANY),
            pl.BlockSpec(memory_space=pl.ANY),
        ],
        out_specs=pl.BlockSpec(memory_space=pltpu.VMEM),
        scratch_shapes=[
            pltpu.VMEM((examples, full_width), gradients.dtype),
            pltpu.SMEM(pair_blocks.shape, pair_blocks.dtype),
            pltpu.VMEM((devices, examples, width), gradients.dtype),
            pltpu.VMEM((devices, packed, taken), jnp.float32),
            pltpu.VMEM((owners, packed, taken), jnp.float32),
            *[pltpu.SemaphoreType.DMA] * 6,
        ],
        compiler_params=pltpu.CompilerParams(collective_id=0, has_side_effects=True),
        name="influence",
    )(gradients[0], pair_blocks)
    return result[None]


def shifted(value, axis, steps):
    count = lax.axis_size(axis)
    pairs = [(source, (source + steps) % count) for source in range(count)]
    return lax.ppermute(value, axis, pairs)


def invert(statistics, example_total):
    traces = jnp.einsum("bpp->b", statistics)
    order = statistics.shape[-1]
    identity = jnp.eye(order, dtype=jnp.float32)
    fisher = (
        statistics / example_total
        + (damping * traces / (order * example_total))[:, None, None] * identity
    )
    factor = jnp.linalg.cholesky(fisher)
    identities = jnp.broadcast_to(identity, fisher.shape)
    factor_inv = lax.linalg.triangular_solve(factor, identities, left_side=True, lower=True)
    return jnp.einsum("bkp,bkq->bpq", factor_inv, factor_inv, precision=lax.Precision.HIGHEST)


def local(gradients, pair_blocks):
    own_rows = gradients[0]
    examples_here, full_width = own_rows.shape
    module_count = full_width // BLOCK_WIDTH
    domain_count = lax.axis_size("domain")
    example_total = examples_here * domain_count * lax.axis_size("shard")
    blocked = own_rows.reshape(examples_here, module_count, BLOCK_WIDTH)
    statistics = jnp.einsum("ibp,ibq->bpq", blocked, blocked, preferred_element_type=jnp.float32)
    partial_sum = lax.psum_scatter(statistics, "shard", scatter_dimension=0, tiled=True)
    partial_sum = lax.psum(partial_sum, "domain")
    inverse = lax.all_gather(invert(partial_sum, example_total), "shard", axis=0, tiled=True)
    precond = jnp.einsum(
        "ibp,bpq->ibq", blocked.astype(jnp.float32), inverse, precision=lax.Precision.HIGHEST
    )
    precond = precond.reshape(examples_here, full_width).astype(jnp.bfloat16)
    inv_root = 1.0 / math.sqrt(full_width)
    domain_index = lax.axis_index("domain")
    row_pieces = []
    for step_by in (-1, 0, 1):
        if step_by == 0:
            row_pieces.append(precond)
        else:
            row_pieces.append(shifted(precond, "shard", step_by))
    queries = jnp.concatenate(row_pieces, 0)
    wide = domain_count * examples_here
    direct = (
        jnp.einsum(
            "ik,jk->ij",
            queries,
            lax.all_gather(own_rows, "domain", axis=0, tiled=True),
            preferred_element_type=jnp.float32,
        )
        * inv_root
    )
    row_blocks = direct.reshape(3, examples_here, wide)
    received = []
    for step_by in (-1, 0, 1):
        if step_by == 0:
            received.append(row_blocks[1])
        else:
            received.append(shifted(row_blocks[step_by + 1], "shard", -step_by))
    final = jnp.stack(received, 0)
    raw_tiles = jnp.transpose(final, (1, 0, 2)).reshape(examples_here, 3 * wide)
    counts = lax.dynamic_index_in_dim(pair_blocks, domain_index, 0, keepdims=False)
    column_all = jnp.arange(3 * wide, dtype=jnp.int32)
    column_domain = column_all // examples_here % domain_count
    limits = jnp.take(counts * (examples_here // COUNT_MAX), column_domain)
    column_index = column_all % examples_here
    row_index = jnp.arange(examples_here, dtype=jnp.int32)
    kept_mask = (row_index[:, None] < limits[None, :]) & (column_index < limits)[None, :]
    return jnp.where(kept_mask, raw_tiles, 0.0)[None]


def solution(mesh):
    placed = (P("domain", "shard", None), P())

    def body(gradients, pair_blocks):
        domain_count, shard_count = mesh.shape["domain"], mesh.shape["shard"]
        devices = domain_count * shard_count
        examples, full_width = gradients.shape[1:]
        columns = len(STEPS) * domain_count * examples
        owner_list = choose_owners(mesh, full_width)
        if owner_list and examples % 8 == 0 and columns <= devices * examples:
            return fused(gradients, pair_blocks, owner_list)
        return local(gradients, pair_blocks)

    return jax.shard_map(
        body, mesh=mesh, in_specs=placed, out_specs=P("domain", "shard", None), check_vma=False
    )
```
